256 devices in a mesh: seq: 32 (over z, y_lo, core), mp: 8 (over y_hi, x).
Axes of the slice: x: 4, y: 4 (y_hi: 2, y_lo: 2; y = y_hi * 2 + y_lo), z: 8, core: 2. Of those that a mesh axis runs over, the one named last changes fastest.
Arguments:
- tokens: bfloat16 [32768, 4096], P('seq', 'mp'), may hold values from -6 to 6
- segment_ids: int32 [32768], P('seq'), may hold values from 0 to 3, never falling along the last dimension, each value on 1 to 16384 neighbouring positions
- w_x: bfloat16 [4096, 4096], P(None, 'mp'), may hold values from -0.09375 to 0.09375
- w_z: bfloat16 [4096, 4096], P(None, 'mp'), may hold values from -0.09375 to 0.09375
- w_bc: bfloat16 [4096, 256], replicated, may hold values from -0.09375 to 0.09375
- w_dt: bfloat16 [4096, 32], P(None, 'mp'), may hold values from -0.09375 to 0.09375
- dt_bias: float32 [32], P('mp'), may hold values from -1 to 1
- rates: float32 [32], P('mp'), may hold values from 1.5258789e-05 to 0.05
- conv_x: float32 [3, 4096], P(None, 'mp'), may hold values from -3 to 3
- conv_bc: float32 [3, 256], replicated, may hold values from -3 to 3
- norm_gain: float32 [4096], P('mp'), may hold values from 0.5 to 1.5
Outputs:
- encoded: bfloat16 [32768, 4096], P('seq', 'mp')
The draws below stay inside these ranges and needn't reach their ends.
Inputs may be any that keep to these rules, and one draw needn't show every extreme that they name: `segment_ids`: document numbers never fall along the slab and start at 0; each document holds 1 to 16384 tokens, and one holds exactly 16384.
All inputs are finite; a program needn't handle non-finite values.
Results may differ from the reference program's by a relative error of at most 0.009.
Values may be sent and summed in bfloat16 or wider, within the bound.
No kernel may reach another device: no remote copies, remote signals or barrier semaphores. Data moves between devices by JAX's collectives and lax.ppermute only.
A program may use at most 128 MiB of HBM per device.

```python
import math
import jax
import jax.numpy as jnp
import numpy as np
from jax import lax

D = 4096
HEADS = 32
HEAD_DIM = 128
STATE = 128
INNER = 4096
TOKENS = 32768
BLOCK = 256


def draw_tokens(key, part):
    base_key = jax.random.fold_in(key, 11)
    level_key = jax.random.fold_in(key, 12)
    region_count = TOKENS // BLOCK
    base = jax.random.normal(base_key, (TOKENS, D), jnp.float32)
    shifts = 1.5 * jax.random.normal(level_key, (region_count, D), jnp.float32)
    offsets = jnp.repeat(shifts, BLOCK, axis=0)
    return jnp.clip(base + offsets, -6.0, 6.0).astype(jnp.bfloat16)


def shard_levels(rng, shape, split, smallest, top_value):
    factor_of, own = 1.0, jax.random.fold_in(rng, 6)
    for axis_at, blocks in split:
        heights = jnp.exp(jax.random.uniform(jax.random.fold_in(own, axis_at), (blocks,), jnp.float32, smallest / len(split), top_value / len(split)))
        factor_of = factor_of * jnp.repeat(heights, shape[axis_at] // blocks).reshape([-1 if axis == axis_at else 1 for axis in range(len(shape))])
    return factor_of


def split_up(number_of, total, most, lean):
    weights = [(1 << 20) // math.isqrt(standing ** lean) + 1 for standing in range(2, number_of + 1)]
    spare, counts = total - most - (number_of - 1), [1] * (number_of - 1)
    while spare > 0:
        movable = [i for i in range(number_of - 1) if counts[i] < most]
        whole, remaining = sum([weights[i] for i in movable]), spare
        for i in movable:
            more = min(most - counts[i], max(1, remaining * weights[i] // whole), spare)
            counts[i] = counts[i] + more
            spare = spare - more
    return np.array([most] + counts)


def ragged(key, amount, total, reach, slope):
    if amount == 2:
        one = jax.random.randint(key, (), max(1, total - reach), min(reach, total - 1) + 1)
        return jnp.stack([one, total - one])
    lengths = jnp.asarray(split_up(amount, total, reach, slope), jnp.int32)
    twos = (amount - 1) // 2
    giver, sink = lengths[1:1 + 2 * twos:2], lengths[2:2 + 2 * twos:2]
    margin = jnp.minimum(giver - 1, reach - sink)
    moved = jax.random.randint(jax.random.fold_in(key, 1), (twos,), 0, 1 << 20) % (margin + 1)
    lengths = lengths.at[1:1 + 2 * twos:2].set(giver - moved).at[2:2 + 2 * twos:2].set(sink + moved)
    return lengths[jax.random.permutation(jax.random.fold_in(key, 2), amount)]


def noise(key, dims, deviation, reach, shards=(), held_as=jnp.bfloat16):
    values = deviation * jax.random.normal(key, dims, jnp.float32)
    if shards:
        values = values * shard_levels(key, dims, shards, -0.22, 0.18)
    return jnp.clip(values, -reach, reach).astype(held_as)


def setup_inputs(seed: int = 0) -> dict:
    seeds = jax.random.split(jax.random.key(seed), 12)
    return {
        "tokens": draw_tokens(jax.random.fold_in(seeds[11], 71), 0),
        "segment_ids": jnp.searchsorted(jnp.cumsum(ragged(seeds[1], 4, TOKENS, TOKENS // 2, 0)), jnp.arange(TOKENS), side="right").astype(jnp.int32),
        "w_x": noise(seeds[2], (D, INNER), D ** -0.5, 0.09375, ((1, 8),)),
        "w_z": noise(seeds[3], (D, INNER), D ** -0.5, 0.09375, ((1, 8),)),
        "w_bc": noise(seeds[4], (D, 2 * STATE), D ** -0.5, 0.09375),
        "w_dt": noise(seeds[5], (D, HEADS), D ** -0.5, 0.09375, ((1, 8),)),
        "dt_bias": jnp.clip(jax.random.uniform(seeds[6], (HEADS,), jnp.float32, -1.0, 1.0) * shard_levels(seeds[6], (HEADS,), ((0, 8),), -0.4, 0.0), -1.0, 1.0),
        "rates": jnp.clip(jnp.exp(math.log(0.05) - 8.094623 * jax.random.uniform(seeds[7], (HEADS,), jnp.float32) ** shard_levels(seeds[7], (HEADS,), ((0, 8),), -0.2, 0.2)), 1.52587890625e-05, 0.05),
        "conv_x": noise(seeds[8], (3, INNER), 0.5, 3.0, ((1, 8),), jnp.float32),
        "conv_bc": noise(seeds[9], (3, 2 * STATE), 0.5, 3.0, (), jnp.float32),
        "norm_gain": jnp.clip(1.0 + 0.1 * jax.random.normal(seeds[10], (INNER,), jnp.float32), 0.5, 1.5),
    }


def rounded(values):
    return lax.optimization_barrier(values.astype(jnp.bfloat16))

def widen(values):
    return lax.optimization_barrier(values).astype(jnp.float32)

def convolve(values, segments, kernel):
    zero_row = jnp.zeros((1, values.shape[1]), jnp.float32)
    padded = jnp.concatenate([zero_row, values, zero_row], axis=0)
    no_doc = jnp.full((1,), -1, jnp.int32)
    seg_pad = jnp.concatenate([no_doc, segments, no_doc])
    before = padded[:-2] * (seg_pad[:-2] == segments)[:, None].astype(jnp.float32)
    after = padded[2:] * (seg_pad[2:] == segments)[:, None].astype(jnp.float32)
    return kernel[0] * before + kernel[1] * values + kernel[2] * after

def sweep(inputs, b_vecs, c_vecs, steps, segments, rates, strict):
    n_tokens = inputs.shape[0]
    n_blocks = n_tokens // BLOCK
    x_blocks = inputs.reshape(n_blocks, BLOCK, HEADS, HEAD_DIM)
    b_blocks = b_vecs.reshape(n_blocks, BLOCK, STATE)
    c_blocks = c_vecs.reshape(n_blocks, BLOCK, STATE)
    dt_blocks = steps.reshape(n_blocks, BLOCK, HEADS)
    seg_blocks = segments.reshape(n_blocks, BLOCK)
    positions = jnp.arange(BLOCK)
    if strict:
        lower_tri = positions[None, :] < positions[:, None]
    else:
        lower_tri = positions[None, :] <= positions[:, None]

    def advance(carry, block_data):
        state_now, seg_prev = carry
        x_blk, b_blk, c_blk, dt_blk, seg_blk = block_data
        cumul = jnp.cumsum(-dt_blk * rates, axis=0)
        keep_mask = (lower_tri & (seg_blk[:, None] == seg_blk[None, :]))[:, :, None]
        gap_sum = cumul[:, None, :] - cumul[None, :, :]
        decay = jnp.where(keep_mask, jnp.exp(jnp.where(keep_mask, gap_sum, 0.0)), 0.0)
        scores = jnp.dot(c_blk, b_blk.T, preferred_element_type=jnp.float32)
        weights = (scores[:, :, None] * decay * dt_blk[None, :, :]).astype(jnp.bfloat16)
        inside = jnp.einsum('ijh,jhp->ihp', widen(weights), x_blk.astype(jnp.float32))
        opening = jnp.where((seg_blk == seg_prev)[:, None], jnp.exp(cumul), 0.0)
        carried = jnp.einsum('in,hpn->ihp', c_blk.astype(jnp.float32), widen(state_now.astype(jnp.bfloat16)))
        carried = carried * opening[:, :, None]
        final_cum = cumul[-1]
        tail_decay = jnp.where((seg_blk == seg_blk[-1])[:, None], jnp.exp(final_cum[None, :] - cumul), 0.0)
        scaled = (x_blk.astype(jnp.float32) * (tail_decay * dt_blk)[:, :, None]).astype(jnp.bfloat16)
        fresh = jnp.einsum('jhp,jn->hpn', widen(scaled), b_blk.astype(jnp.float32))
        block_decay = jnp.exp(final_cum) * (seg_blk[-1] == seg_prev).astype(jnp.float32)
        state_next = block_decay[:, None, None] * state_now + fresh
        return ((state_next, seg_blk[-1]), inside + carried)
    start_state = (jnp.zeros((HEADS, HEAD_DIM, STATE), jnp.float32), jnp.array(-1, jnp.int32))
    _, outputs = lax.scan(advance, start_state, (x_blocks, b_blocks, c_blocks, dt_blocks, seg_blocks))
    return outputs.reshape(n_tokens, HEADS * HEAD_DIM)

def reference(tokens, segment_ids, w_x, w_z, w_bc, w_dt, dt_bias, rates, conv_x, conv_bc, norm_gain):
    proj_x = rounded(jnp.dot(tokens, w_x, preferred_element_type=jnp.float32))
    gate = rounded(jnp.dot(tokens, w_z, preferred_element_type=jnp.float32))
    proj_bc = rounded(jnp.dot(tokens, w_bc, preferred_element_type=jnp.float32))
    steps = jax.nn.softplus(jnp.dot(tokens, w_dt, preferred_element_type=jnp.float32) + dt_bias)
    inputs = rounded(jax.nn.silu(convolve(proj_x.astype(jnp.float32), segment_ids, conv_x)))
    vectors = rounded(jax.nn.silu(convolve(proj_bc.astype(jnp.float32), segment_ids, conv_bc)))
    b_vecs = vectors[:, :STATE]
    c_vecs = vectors[:, STATE:]
    forward = sweep(inputs, b_vecs, c_vecs, steps, segment_ids, rates, False)
    backward = sweep(inputs[::-1], b_vecs[::-1], c_vecs[::-1], steps[::-1], segment_ids[::-1], rates, True)[::-1]
    mixed_y = forward + backward
    gated = mixed_y * jax.nn.silu(gate.astype(jnp.float32))
    scale = lax.rsqrt(lax.optimization_barrier(jnp.mean(gated * gated, axis=1, keepdims=True)) + 1e-05)
    return (gated * scale * norm_gain).astype(jnp.bfloat16)
```

```python
import functools

import jax
import jax.numpy as jnp
from jax import lax
from jax.experimental import pallas as pl
from jax.experimental.pallas import tpu as pltpu
from jax.sharding import PartitionSpec as P

BF16 = jnp.bfloat16
F32 = jnp.float32
BLOCK = 256
LANES = 128
HALO = 16
ANY = pl.BlockSpec(memory_space=pl.ANY)
LIMIT = 48 << 20


def silu(v):
    half = 0.5 * v
    return half + half * jnp.tanh(half)


def dot(a, b):
    return jnp.dot(a, b, preferred_element_type=F32)


def params():
    return pltpu.CompilerParams(vmem_limit_bytes=LIMIT)


def fetch_plan(count, split, rows):
    plan = []
    for slot in range(count):
        if slot in split:
            plan += [(slot, 0, rows // 2), (slot, rows // 2, rows // 2)]
        else:
            plan.append((slot, 0, rows))
    return plan


def load_pieces(step, plan, refs, buf, sems, extra=()):
    copies = [
        pltpu.make_async_copy(ref, buf.at[slot, pl.ds(at, rows)], sems.at[i])
        for i, (ref, (slot, at, rows)) in enumerate(zip(refs, plan))
    ]
    more = [(slot, pltpu.make_async_copy(src, dst, sems.at[len(refs) + i])) for i, (slot, src, dst) in enumerate(extra)]

    @pl.when(step == 0)
    def _():
        for c in copies:
            c.start()
        for _, c in more:
            c.start()

    for slot in range(1 + max(p[0] for p in plan)):

        @pl.when(step == slot)
        def _(slot=slot):
            for c, p in zip(copies, plan):
                if p[0] == slot:
                    c.wait()
            for s, c in more:
                if s == slot:
                    c.wait()


def project_kernel(plan, rows, halo, idx, *refs):
    n = len(plan)
    pieces = refs[:n]
    refs = refs[n:]
    extra = ()
    if halo:
        edge, refs = refs[0], refs[1:]
    wx, wb, wd, bias, xo, bo, do, buf, ax, ab, ad, sems = refs
    step = pl.program_id(0)
    if halo:
        extra = [(k, edge.at[idx[k]], buf.at[k, pl.ds(rows, HALO)]) for k in range(8)]
    load_pieces(step, plan, pieces, buf, sems, extra)

    lhs = buf[step]
    px, pb, pd = dot(lhs, wx[...]), dot(lhs, wb[...]), dot(lhs, wd[...])

    @pl.when(step == 0)
    def _():
        ax[...] = px
        ab[...] = pb
        ad[...] = pd

    @pl.when(step > 0)
    def _():
        ax[...] += px
        ab[...] += pb
        ad[...] += pd

    @pl.when(step == pl.num_programs(0) - 1)
    def _():
        xo[...] = ax[...].astype(BF16)
        bo[...] = ab[...].astype(BF16)
        v = ad[...] + bias[...]
        do[...] = jnp.maximum(v, 0.0) + jnp.log1p(jnp.exp(-jnp.abs(v)))


def project(idx, plan, pieces, edge, wx, wb, wd, bias):
    rows = pieces[0].shape[0]
    depth = pieces[0].shape[1]
    halo = edge is not None
    total = rows + (HALO if halo else 0)
    nx, nb = wx.shape[1], wb.shape[1]
    count = 8
    args = list(pieces) + ([edge] if halo else [])
    return pl.pallas_call(
        functools.partial(project_kernel, plan, rows, halo),
        grid_spec=pltpu.PrefetchScalarGridSpec(
            num_scalar_prefetch=1,
            grid=(count,),
            in_specs=[ANY] * len(args)
            + [
                pl.BlockSpec((depth, nx), lambda k, i: (i[k], 0)),
                pl.BlockSpec((depth, nb), lambda k, i: (i[k], 0)),
                pl.BlockSpec((depth, LANES), lambda k, i: (i[k], 0)),
                pl.BlockSpec((1, LANES), lambda k, i: (0, 0)),
            ],
            out_specs=[
                pl.BlockSpec((total, nx), lambda k, i: (0, 0)),
                pl.BlockSpec((total, nb), lambda k, i: (0, 0)),
                pl.BlockSpec((total, LANES), lambda k, i: (0, 0)),
            ],
            scratch_shapes=[
                pltpu.VMEM((count, total, depth), BF16),
                pltpu.VMEM((total, nx), F32),
                pltpu.VMEM((total, nb), F32),
                pltpu.VMEM((total, LANES), F32),
                pltpu.SemaphoreType.DMA((len(plan) + (8 if halo else 0),)),
            ],
        ),
        out_shape=[
            jax.ShapeDtypeStruct((total, nx), BF16),
            jax.ShapeDtypeStruct((total, nb), BF16),
            jax.ShapeDtypeStruct((total, LANES), F32),
        ],
        compiler_params=params(),
        cost_estimate=pl.CostEstimate(
            flops=2 * total * depth * count * (nx + nb + LANES),
            bytes_accessed=2 * depth * count * (total + nx + nb),
            transcendentals=0,
        ),
        name="project",
    )(idx, *args, wx, wb, wd, bias)


def gate_kernel(plan, rows, idx, *refs):
    n = len(plan)
    pieces = refs[:n]
    wz, out, buf, acc, sems = refs[n:]
    step = pl.program_id(0)
    load_pieces(step, plan, pieces, buf, sems)
    part = dot(buf[step], wz[...])

    @pl.when(step == 0)
    def _():
        acc[...] = part

    @pl.when(step > 0)
    def _():
        acc[...] += part

    @pl.when(step == pl.num_programs(0) - 1)
    def _():
        out[...] = silu(acc[...].astype(BF16).astype(F32))


def gate_project(idx, plan, pieces, wz, rows):
    depth = pieces[0].shape[1]
    nz = wz.shape[1]
    count = 8
    return pl.pallas_call(
        functools.partial(gate_kernel, plan, rows),
        grid_spec=pltpu.PrefetchScalarGridSpec(
            num_scalar_prefetch=1,
            grid=(count,),
            in_specs=[ANY] * len(pieces) + [pl.BlockSpec((depth, nz), lambda k, i: (i[k], 0))],
            out_specs=pl.BlockSpec((rows, nz), lambda k, i: (0, 0)),
            scratch_shapes=[
                pltpu.VMEM((count, rows, depth), BF16),
                pltpu.VMEM((rows, nz), F32),
                pltpu.SemaphoreType.DMA((len(plan),)),
            ],
        ),
        out_shape=jax.ShapeDtypeStruct((rows, nz), F32),
        compiler_params=params(),
        cost_estimate=pl.CostEstimate(
            flops=2 * rows * depth * count * nz, bytes_accessed=2 * depth * count * (rows + nz), transcendentals=0
        ),
        name="gate",
    )(idx, *pieces, wz)


def triangle():
    at = lax.broadcasted_iota(jnp.int32, (BLOCK, BLOCK), 0)
    before = lax.broadcasted_iota(jnp.int32, (BLOCK, BLOCK), 1)
    return before <= at


def running(dt, rates):
    a = -dt * rates
    cf = jnp.dot(triangle().astype(F32), a, precision=lax.Precision.HIGHEST, preferred_element_type=F32)
    return a, cf, cf - a


def spread(row, heads):
    return jnp.concatenate([jnp.broadcast_to(row[:, h : h + 1], (row.shape[0], LANES)) for h in range(heads)], axis=1)


def weigh(values, weights, heads):
    return jnp.concatenate(
        [values[:, h * LANES : (h + 1) * LANES] * weights[:, h : h + 1] for h in range(heads)], axis=1
    )


def state_kernel(heads, xa, xb, ba, bb, da, db, kx, kb, cols, links, rates, xs, bcs, dts, pay, loc, dec, xf, bf):
    half = xb.shape[0]
    blocks = 2 * half // BLOCK
    for dst, lo, hi in ((xf, xa, xb), (bf, ba, bb)):
        dst[8 : 8 + half] = lo[:half].astype(F32)
        dst[8 + half : 8 + 2 * half] = hi[...].astype(F32)
        edge = lo[half : half + HALO].astype(F32)
        dst[7:8] = edge[0:1]
        dst[8 + 2 * half : 9 + 2 * half] = edge[1:2]
    dts[:half] = da[:half]
    dts[half:] = db[...]
    rate = rates[...]
    sums = []
    for b in range(blocks):
        at = b * BLOCK
        col = cols[at : at + BLOCK]
        same_prev, same_next = col[:, 0:1], col[:, 1:2]

        def conv(src, taps):
            base = 8 + at
            before = src[base - 1 : base - 1 + BLOCK] * same_prev
            after = src[base + 1 : base + 1 + BLOCK] * same_next
            return silu(taps[0:1] * before + taps[1:2] * src[base : base + BLOCK] + taps[2:3] * after)

        x_blk = conv(xf, kx).astype(BF16)
        bc_blk = conv(bf, kb).astype(BF16)
        xs[at : at + BLOCK] = x_blk
        bcs[at : at + BLOCK] = bc_blk
        x_f = x_blk.astype(F32)
        b_t = bc_blk[:, :LANES].astype(F32).T.astype(BF16)
        dt = dts[at : at + BLOCK]
        a, cf, ce = running(dt, rate)
        last = cf[BLOCK - 1 : BLOCK]
        wf = jnp.exp(last - cf) * col[:, 2:3] * dt
        wb = jnp.exp(ce) * col[:, 3:4] * dt
        loc[0, b] = dot(b_t, weigh(x_f, wf, heads).astype(BF16))
        loc[1, b] = dot(b_t, weigh(x_f, wb, heads).astype(BF16))
        sums.append(jnp.exp(last))
    zero = jnp.zeros((loc.shape[2], loc.shape[3]), F32)
    link = links[...]
    for way in range(2):
        total = jnp.ones((1, LANES), F32)
        state = zero
        for i in range(blocks):
            b = i if way == 0 else blocks - 1 - i
            fresh = loc[way, b]
            loc[way, b] = state
            dec[way, b : b + 1] = spread(total, heads)
            step = sums[b] * link[way : way + 1, b : b + 1]
            state = spread(step, heads) * state + fresh
            total = total * step
        rows = state.shape[0]
        pay[way * rows : (way + 1) * rows, : state.shape[1]] = state.astype(BF16)
        high = total.astype(BF16).astype(F32)
        low = total - high
        eight = jnp.concatenate(
            [jnp.broadcast_to(p[:, h : h + 1], (1, LANES)) for p in (high, low) for h in range(heads)], axis=0
        ).astype(BF16)
        pair = jnp.concatenate([eight, eight], axis=0)
        for j in range(rows // 16):
            pay[way * rows + 16 * j : way * rows + 16 * j + 16, state.shape[1] :] = pair


def states(heads, xa, xb, ba, bb, da, db, kx, kb, cols, links, rates):
    rows = 2 * xb.shape[0]
    nx, nb = xb.shape[1], bb.shape[1]
    blocks = rows // BLOCK
    return pl.pallas_call(
        functools.partial(state_kernel, heads),
        out_shape=[
            jax.ShapeDtypeStruct((rows, nx), BF16),
            jax.ShapeDtypeStruct((rows, nb), BF16),
            jax.ShapeDtypeStruct((rows, LANES), F32),
            jax.ShapeDtypeStruct((2 * LANES, nx + LANES), BF16),
            jax.ShapeDtypeStruct((2, blocks, LANES, nx), F32),
            jax.ShapeDtypeStruct((2, blocks, nx), F32),
        ],
        scratch_shapes=[pltpu.VMEM((rows + 16, nx), F32), pltpu.VMEM((rows + 16, nb), F32)],
        compiler_params=params(),
        name="states",
    )(xa, xb, ba, bb, da, db, kx, kb, cols, links, rates)


def scan_kernel(heads, flag, src, out):
    count = src.shape[0]
    width = out.shape[2]
    ahead = flag[0] == 1

    def one(i, state):
        q = jnp.where(ahead, i, count - 1 - i)
        out[q] = state.astype(BF16)
        got = src[q].astype(F32)
        d = jnp.concatenate(
            [got[h : h + 1, width:] + got[heads + h : heads + h + 1, width:] for h in range(heads)], axis=1
        )
        return d * state + got[:, :width]

    lax.fori_loop(0, count, one, jnp.zeros((out.shape[1], width), F32), unroll=4)


def scan(heads, flag, src, width):
    return pl.pallas_call(
        functools.partial(scan_kernel, heads),
        in_specs=[pl.BlockSpec(memory_space=pltpu.SMEM), pl.BlockSpec(memory_space=pltpu.VMEM)],
        out_shape=jax.ShapeDtypeStruct((src.shape[0], src.shape[1], width), BF16),
        compiler_params=params(),
        name="scan",
    )(flag, src)


def inside_kernel(heads, xs, bcs, dts, cols, rowseg, rates, out):
    dt = dts[...]
    a, cf, ce = running(dt, rates[...])
    cf_r, ce_r, dt_r = cf.T, ce.T, dt.T
    bc = bcs[...]
    b_t = bc[:, :LANES].astype(F32).T.astype(BF16)
    scores = dot(bc[:, LANES:], b_t)
    same = cols[...][:, 6:7] == rowseg[0]
    scores = jnp.where(same, scores, 0.0)
    lower = triangle()
    x = xs[...]
    for h in range(heads):
        gap = jnp.where(lower, cf[:, h : h + 1] - cf_r[h : h + 1], ce_r[h : h + 1] - ce[:, h : h + 1])
        w = (scores * jnp.exp(gap) * dt_r[h : h + 1]).astype(BF16)
        out[:, h * LANES : (h + 1) * LANES] = dot(w, x[:, h * LANES : (h + 1) * LANES])


def inside(heads, xs, bcs, dts, cols, rowseg, rates):
    rows, nx = xs.shape
    nb = bcs.shape[1]
    row = lambda width: pl.BlockSpec((BLOCK, width), lambda b: (b, 0))
    return pl.pallas_call(
        functools.partial(inside_kernel, heads),
        grid=(rows // BLOCK,),
        in_specs=[
            row(nx),
            row(nb),
            row(LANES),
            row(cols.shape[1]),
            pl.BlockSpec((1, 1, BLOCK), lambda b: (b, 0, 0)),
            pl.BlockSpec((1, LANES), lambda b: (0, 0)),
        ],
        out_specs=row(nx),
        out_shape=jax.ShapeDtypeStruct((rows, nx), F32),
        compiler_params=params(),
        cost_estimate=pl.CostEstimate(
            flops=2 * rows * BLOCK * (nx + LANES), bytes_accessed=rows * nx * 6, transcendentals=rows * BLOCK * heads
        ),
        name="inside",
    )(xs, bcs, dts, cols, rowseg, rates)


def finish_kernel(heads, enter, loc, dec, y_in, sg, bcs, dts, cols, rates, out, ss):
    b = pl.program_id(0)
    dt = dts[...]
    a, cf, ce = running(dt, rates[...])
    last = cf[BLOCK - 1 : BLOCK]
    col = cols[...]
    open_f = jnp.exp(cf) * col[:, 4:5]
    open_b = jnp.exp(last - ce) * col[:, 5:6]
    c = bcs[...][:, LANES:]
    y = y_in[...]
    for way, opening in ((0, open_f), (1, open_b)):
        held = dec[way, b][None] * enter[way * LANES : (way + 1) * LANES].astype(F32) + loc[way, 0]
        y = y + weigh(dot(c, held.astype(BF16)), opening, heads)
    gated = y * sg[...]
    out[...] = gated
    sq = gated * gated
    part = sq[:, :LANES]
    for h in range(1, heads):
        part = part + sq[:, h * LANES : (h + 1) * LANES]
    ss[0] = jnp.sum(part.T, axis=0, keepdims=True)


def finish(heads, enter, loc, dec, y_in, sg, bcs, dts, cols, rates):
    rows, nx = y_in.shape
    nb = bcs.shape[1]
    blocks = rows // BLOCK
    row = lambda width: pl.BlockSpec((BLOCK, width), lambda b: (b, 0))
    return pl.pallas_call(
        functools.partial(finish_kernel, heads),
        grid=(blocks,),
        in_specs=[
            pl.BlockSpec(enter.shape, lambda b: (0, 0)),
            pl.BlockSpec((2, 1, LANES, nx), lambda b: (0, b, 0, 0)),
            pl.BlockSpec(dec.shape, lambda b: (0, 0, 0)),
            row(nx),
            row(nx),
            row(nb),
            row(LANES),
            row(cols.shape[1]),
            pl.BlockSpec((1, LANES), lambda b: (0, 0)),
        ],
        out_specs=[row(nx), pl.BlockSpec((1, 1, BLOCK), lambda b: (b, 0, 0))],
        out_shape=[jax.ShapeDtypeStruct((rows, nx), F32), jax.ShapeDtypeStruct((blocks, 1, BLOCK), F32)],
        compiler_params=params(),
        name="finish",
    )(enter, loc, dec, y_in, sg, bcs, dts, cols, rates)


def scale_kernel(columns, gated, gain, *refs):
    parts, out = refs[:-1], refs[-1]
    total = parts[0][0]
    for p in parts[1:]:
        total = total + p[0]
    scale = lax.rsqrt(total / columns + 1e-05)
    col = jnp.broadcast_to(scale, (LANES, BLOCK)).T[:, 0:1]
    out[...] = (gated[...] * col * gain[...]).astype(BF16)


def scale(columns, gated, gain, parts):
    rows, nx = gated.shape
    row = pl.BlockSpec((BLOCK, nx), lambda b: (b, 0))
    part = pl.BlockSpec((1, 1, BLOCK), lambda b: (b, 0, 0))
    return pl.pallas_call(
        functools.partial(scale_kernel, columns),
        grid=(rows // BLOCK,),
        in_specs=[row, pl.BlockSpec((1, nx), lambda b: (0, 0))] + [part] * len(parts),
        out_specs=row,
        out_shape=jax.ShapeDtypeStruct((rows, nx), BF16),
        compiler_params=params(),
        name="scale",
    )(gated, gain, *parts)


def shards(tokens, segment_ids, w_x, w_z, w_bc, w_dt, dt_bias, rates, conv_x, conv_bc, norm_gain):
    rows, depth = tokens.shape
    heads = w_dt.shape[1]
    nx = w_x.shape[1]
    blocks = rows // BLOCK
    mp, seq = lax.axis_size("mp"), lax.axis_size("seq")
    ring = mp // 2
    me = lax.axis_index("mp")
    row_at, col_at = me // ring, me % ring
    turn = lambda s: [(r * ring + c, r * ring + (c + s) % ring) for r in range(2) for c in range(ring)]
    send = lambda v, pairs: lax.ppermute(v, "mp", pairs)
    right, left = turn(1), turn(-1)
    across = [(i, (i + ring) % mp) for i in range(mp)]
    half = rows // 2
    quarter = half // 2

    first = []
    for i in range(2):
        own = tokens[i * half : (i + 1) * half]
        first.append((own, send(own, right), send(own, left), send(own, across)))
    pieces = []
    for own, r1, l1, p in first:
        o1, o2 = send(r1[:quarter], right), send(l1[quarter:], left)
        pr, pll = send(p, right), send(p, left)
        po1, po2 = send(o1, across), send(o2, across)
        pieces.append([own, r1, l1, p, o1, o2, pr, pll, po1, po2])
    plan = fetch_plan(8, (4, 7), half)
    idx = jnp.stack(
        [r * ring + (col_at + s) % ring for r, s in (
            (row_at, 0), (row_at, -1), (row_at, 1), (1 - row_at, 0),
            (row_at, 2), (1 - row_at, -1), (1 - row_at, 1), (1 - row_at, 2))]
    ).astype(jnp.int32)

    seg = segment_ids.astype(F32) + 1.0
    tail = jnp.concatenate([tokens[rows - 1 :], jnp.broadcast_to(seg[rows - 1 :, None], (1, LANES)).astype(BF16)], axis=1)
    head = jnp.concatenate([tokens[:1], jnp.broadcast_to(seg[:1, None], (1, LANES)).astype(BF16)], axis=1)
    before = lax.ppermute(tail, "seq", [(i, i + 1) for i in range(seq - 1)])
    after = lax.ppermute(head, "seq", [(i + 1, i) for i in range(seq - 1)])
    left_seg = before[0, depth].astype(F32)
    right_seg = after[0, depth].astype(F32)
    edge = jnp.concatenate([before[:, :depth], after[:, :depth], jnp.zeros((HALO - 2, depth), BF16)], axis=0)
    edge = lax.all_to_all(jnp.broadcast_to(edge[None], (mp, HALO, depth)), "mp", 0, 0)

    prev = jnp.concatenate([left_seg[None], seg[:-1]])
    nxt = jnp.concatenate([seg[1:], right_seg[None]])
    by = seg.reshape(blocks, BLOCK)
    ends, starts = by[:, -1], by[:, 0]
    prev_end = jnp.concatenate([left_seg[None], ends[:-1]])
    next_start = jnp.concatenate([starts[1:], right_seg[None]])
    wide = lambda v: jnp.broadcast_to(v[:, None], (blocks, BLOCK)).reshape(rows)
    cols = jnp.stack(
        [
            (seg == prev).astype(F32),
            (seg == nxt).astype(F32),
            (seg == wide(ends)).astype(F32),
            (seg == wide(starts)).astype(F32),
            (seg == wide(prev_end)).astype(F32),
            (seg == wide(next_start)).astype(F32),
            seg,
            seg,
        ],
        axis=1,
    )
    links = jnp.stack([(ends == prev_end).astype(F32), (starts == next_start).astype(F32)])
    rowseg = by[:, None, :]
    rate = jnp.pad(rates, (0, LANES - heads))[None]
    bias = jnp.pad(dt_bias, (0, LANES - heads))[None]
    w_d = jnp.pad(w_dt, ((0, 0), (0, LANES - heads)))

    xa, ba, da = project(idx, plan, pieces[0], edge, w_x, w_bc, w_d, bias)
    xb, bb, db = project(idx, plan, pieces[1], None, w_x, w_bc, w_d, bias)
    xs, bcs, dts, pay, loc, dec = states(heads, xa, xb, ba, bb, da, db, conv_x, conv_bc, cols, links, rate)

    width = nx
    got = lax.all_to_all(pay.reshape(seq, 2 * LANES // seq, width + LANES), "seq", 0, 0)
    flag = (lax.axis_index("seq") < seq // 2).astype(jnp.int32)[None]
    entered = scan(heads, flag, got, width)
    enter = lax.all_to_all(entered, "seq", 0, 0).reshape(2 * LANES, width)

    y_in = inside(heads, xs, bcs, dts, cols, rowseg, rate)
    sg = jnp.concatenate([gate_project(idx, plan, p, w_z, half) for p in pieces], axis=0)

    gated, ss = finish(heads, enter, loc, dec, y_in, sg, bcs, dts, cols, rate)
    ss = ss + send(ss, across)
    parts = [ss] + [send(ss, turn(s)) for s in range(1, ring)]
    return scale(nx * mp, gated, norm_gain[None], parts)


def solution(mesh):
    placed = (
        P("seq", "mp"),
        P("seq"),
        P(None, "mp"),
        P(None, "mp"),
        P(),
        P(None, "mp"),
        P("mp"),
        P("mp"),
        P(None, "mp"),
        P(),
        P("mp"),
    )
    return jax.shard_map(
        shards, mesh=mesh, in_specs=placed, out_specs=P("seq", "mp"), check_vma=False
    )
```

```python
import functools

import jax
import jax.numpy as jnp
from jax import lax
from jax.experimental import pallas as pl
from jax.experimental.pallas import tpu as pltpu
from jax.sharding import PartitionSpec as P

BF16 = jnp.bfloat16
F32 = jnp.float32
BLOCK = 256
LANES = 128
SUB = 8
ANY = pl.BlockSpec(memory_space=pl.ANY)
VMEM = pl.BlockSpec(memory_space=pltpu.VMEM)
SMEM = pl.BlockSpec(memory_space=pltpu.SMEM)


def silu(v):
    half = 0.5 * v
    return half + half * jnp.tanh(half)


def dot(a, b):
    return jnp.dot(a, b, preferred_element_type=F32)


def params(mib):
    return pltpu.CompilerParams(vmem_limit_bytes=mib << 20)


def far(*arrays):
    return [pltpu.with_memory_space_constraint(a, pltpu.HBM) for a in arrays]


def fetch(pairs, sems):
    copies = [pltpu.make_async_copy(src, dst, sems.at[i]) for i, (src, dst) in enumerate(pairs)]
    for c in copies:
        c.start()
    return copies


def rows_of(ref, idx, k, depth):
    return ref.at[pl.ds(pl.multiple_of(idx[k] * depth, depth), depth)]


def nt_dot(a, b):
    return lax.dot_general(a, b, (((1,), (1,)), ((), ())), preferred_element_type=F32)


def place(plan, pieces, buf):
    return [(slot, ref, buf.at[slot, pl.ds(at, rows)]) for ref, (slot, at, rows) in zip(pieces, plan)]


def plan_of(pieces, keep=None):
    whole = max(p.shape[0] for p in pieces)
    full = keep or whole
    plan, slot, at = [], 0, 0
    for p in pieces:
        rows = min(p.shape[0], full - at)
        plan.append((slot, at, rows))
        at += p.shape[0]
        if at == whole:
            slot, at = slot + 1, 0
    return tuple(plan), slot


def multiply(slots, plan, idx, pieces, weights, wd, buf, views, sems, sums):
    depth = buf.shape[2]
    order_of = [[] for _ in slots]
    pairs = []
    for i, k in enumerate(slots):
        for w, v in zip(weights, views):
            order_of[i].append(len(pairs))
            pairs.append((rows_of(w, idx, k, depth), v.at[i]))
        for ref, (slot, at, rows) in zip(pieces, plan):
            if slot == i:
                order_of[i].append(len(pairs))
                pairs.append((ref.at[pl.ds(0, rows)], buf.at[i, pl.ds(at, rows)]))
    copies = fetch(pairs, sems)
    for i, k in enumerate(slots):
        for c in order_of[i]:
            copies[c].wait()
        lhs = buf[i]
        parts = [dot(lhs, v[i]) for v in views]
        if wd is not None:
            parts.append(nt_dot(wd[:, pl.ds(pl.multiple_of(idx[k] * depth, depth), depth)], lhs))
        sums = [p if s is None else s + p for s, p in zip(sums, parts)]
    return sums


def step_sizes(v, bias):
    v = v[:SUB] + bias[:SUB]
    return jnp.maximum(v, 0.0) + jnp.log1p(jnp.exp(-jnp.abs(v)))


def project_kernel(slots, plan, last, idx, *refs):
    n = len(plan)
    pieces, refs = refs[:n], refs[n:]
    wx, wb, wd, bias = refs[:4]
    outs, (buf, vx, vb, sems) = refs[4:7], refs[7:]
    sums = multiply(slots, plan, idx, pieces, (wx, wb), wd, buf, (vx, vb), sems, [None] * 3)
    if last:
        outs[0][...] = sums[0].astype(BF16)
        outs[1][...] = sums[1].astype(BF16)
        outs[2][...] = step_sizes(sums[2], bias[...][:, 0:1])
    else:
        for o, s in zip(outs, sums):
            o[...] = s


def scratch_of(n, rows, depth, widths, copies):
    return (
        [pltpu.VMEM((n, rows, depth), BF16)]
        + [pltpu.VMEM((n, depth, w), BF16) for w in widths]
        + [pltpu.SemaphoreType.DMA((copies,))]
    )


def project(idx, slots, pieces, wx, wb, wd, bias, last):
    rows, depth = max(p.shape[0] for p in pieces), pieces[0].shape[1]
    plan, n = plan_of(pieces)
    nx, nb, nd = wx.shape[1], wb.shape[1], wd.shape[0]
    kind = BF16 if last else F32
    return pl.pallas_call(
        functools.partial(project_kernel, slots, plan, last),
        in_specs=[SMEM] + [ANY] * (len(pieces) + 2) + [VMEM, VMEM],
        out_specs=[VMEM] * 3,
        scratch_shapes=scratch_of(n, rows, depth, (nx, nb), 2 * n + len(pieces)),
        out_shape=[
            jax.ShapeDtypeStruct((rows, nx), kind),
            jax.ShapeDtypeStruct((rows, nb), kind),
            jax.ShapeDtypeStruct((SUB if last else nd, rows), F32),
        ],
        compiler_params=params(24),
        cost_estimate=pl.CostEstimate(
            flops=2 * rows * depth * n * (nx + nb + LANES),
            bytes_accessed=2 * depth * n * (rows + nx + nb),
            transcendentals=0,
        ),
        name="project",
    )(idx, *far(*pieces, wx, wb), wd, bias)


def gate_kernel(plan_a, plan_b, idx, *refs):
    na, nb = len(plan_a), len(plan_b)
    pieces_a, pieces_b, (wz, out, buf, vz, sems) = refs[:na], refs[na : na + nb], refs[na + nb :]
    half = out.shape[0] // 2
    n, depth = buf.shape[0], buf.shape[2]
    plan = [(s, at, r) for s, at, r in plan_a] + [(s, at + half, r) for s, at, r in plan_b]
    (total,) = multiply(
        tuple(range(n)), plan, idx, pieces_a + pieces_b, (wz,), None, buf, (vz,), sems, [None]
    )
    out[...] = silu(total.astype(BF16).astype(F32))


def gate_project(idx, pieces_a, pieces_b, wz):
    half, depth = pieces_a[0].shape
    nz = wz.shape[1]
    plan_a, n = plan_of(pieces_a)
    plan_b, _ = plan_of(pieces_b, half)
    count = len(plan_a) + len(plan_b)
    return pl.pallas_call(
        functools.partial(gate_kernel, plan_a, plan_b),
        in_specs=[SMEM] + [ANY] * (count + 1),
        out_specs=VMEM,
        scratch_shapes=scratch_of(n, 2 * half, depth, (nz,), n + count),
        out_shape=pltpu.HBM((2 * half, nz), F32),
        compiler_params=params(28),
        cost_estimate=pl.CostEstimate(
            flops=4 * half * depth * n * nz, bytes_accessed=2 * depth * n * (2 * half + nz), transcendentals=0
        ),
        name="gate",
    )(idx, *far(*pieces_a, *pieces_b, wz))


def order(strict=False):
    at = lax.broadcasted_iota(jnp.int32, (BLOCK, BLOCK), 0)
    to = lax.broadcasted_iota(jnp.int32, (BLOCK, BLOCK), 1)
    return at, to


def running(dt, rates):
    at, to = order()
    a = -dt * rates
    cf = jnp.dot(a, (at <= to).astype(F32), precision=lax.Precision.HIGHEST, preferred_element_type=F32)
    return cf, cf - a


def columns(*groups):
    zero = jnp.zeros((LANES - SUB * len(groups), BLOCK), F32)
    return jnp.concatenate([*groups, zero], axis=0).T


def equal(a, b):
    return (a == b).astype(F32)


def marks(segs):
    seg, prev, nxt = segs[0:1], segs[1:2], segs[2:3]
    return seg, prev, nxt, seg[:, :1], seg[:, BLOCK - 1 :], prev[:, :1], nxt[:, BLOCK - 1 :]


def spread(col, heads):
    return jnp.concatenate([jnp.broadcast_to(col[h : h + 1], (1, LANES)) for h in range(heads)], axis=1)


def weigh(values, weights, at, heads):
    return jnp.concatenate(
        [values[:, h * LANES : (h + 1) * LANES] * weights[:, at + h : at + h + 1] for h in range(heads)], axis=1
    )


def state_kernel(heads, slots, plan, idx, *refs):
    n = len(plan)
    pieces, refs = refs[:n], refs[n:]
    wx, wb, wd, bias, hx, hb, hd, xa, ba, da, kx, kb, segs, rates = refs[:14]
    xs, bcs, dts, pay, loc, dec = refs[14:20]
    buf, vx, vb, sems, xf, bf = refs[20:]
    half = xa.shape[0]
    blocks = 2 * half // BLOCK
    xf[8 : 8 + half] = xa[...].astype(F32)
    bf[8 : 8 + half] = ba[...].astype(F32)
    sums = multiply(slots, plan, idx, pieces, (wx, wb), wd, buf, (vx, vb), sems, [hx[...], hb[...], hd[...]])
    for dst, full in ((xf, sums[0]), (bf, sums[1])):
        full = full.astype(BF16).astype(F32)
        dst[8 + half : 8 + 2 * half] = full[:half]
        edge = full[half:]
        dst[7:8] = edge[SUB - 1 : SUB]
        dst[8 + 2 * half : 9 + 2 * half] = edge[SUB : SUB + 1]
    dts[:, :half] = da[...]
    dts[:, half:] = step_sizes(sums[2], bias[...][:, 0:1])[:, :half]
    rate = rates[...][:, 0:1]
    steps = []
    for b in range(blocks):
        at = b * BLOCK
        seg, prev, nxt, start, end, prev_end, next_start = marks(segs[:, at : at + BLOCK])
        dt = dts[:, at : at + BLOCK]
        cf, ce = running(dt, rate)
        last = cf[:, BLOCK - 1 :]
        wide = lambda row: jnp.broadcast_to(row, (SUB, BLOCK))
        col = columns(
            jnp.exp(last - cf) * dt * equal(seg, end),
            jnp.exp(ce) * dt * equal(seg, start),
            wide(equal(seg, prev)),
            wide(equal(seg, nxt)),
        )
        steps.append((jnp.exp(last) * equal(end, prev_end), jnp.exp(last) * equal(start, next_start)))
        same_prev, same_next = col[:, 2 * SUB : 2 * SUB + 1], col[:, 3 * SUB : 3 * SUB + 1]

        def conv(src, taps):
            base = 8 + at
            before = src[base - 1 : base - 1 + BLOCK] * same_prev
            after = src[base + 1 : base + 1 + BLOCK] * same_next
            return silu(taps[0:1] * before + taps[1:2] * src[base : base + BLOCK] + taps[2:3] * after)

        x_blk = conv(xf, kx).astype(BF16)
        bc_blk = conv(bf, kb).astype(BF16)
        xs[at : at + BLOCK] = x_blk
        bcs[at : at + BLOCK] = bc_blk
        x_f = x_blk.astype(F32)
        b_t = bc_blk[:, :LANES].astype(F32).T.astype(BF16)
        loc[0, b] = dot(b_t, weigh(x_f, col, 0, heads).astype(BF16))
        loc[1, b] = dot(b_t, weigh(x_f, col, SUB, heads).astype(BF16))
    for way in range(2):
        total = jnp.ones((SUB, 1), F32)
        state = jnp.zeros((loc.shape[2], loc.shape[3]), F32)
        for i in range(blocks):
            b = i if way == 0 else blocks - 1 - i
            fresh = loc[way, b]
            loc[way, b] = state
            dec[way, b : b + 1] = spread(total, heads)
            step = steps[b][way]
            state = spread(step, heads) * state + fresh
            total = total * step
        rows, width = state.shape
        pay[way * rows : (way + 1) * rows, :width] = state.astype(BF16)
        high = total[:heads].astype(BF16).astype(F32)
        both = jnp.concatenate([high, total[:heads] - high], axis=0)
        eight = jnp.broadcast_to(both, (2 * heads, LANES)).astype(BF16)
        pair = jnp.concatenate([eight, eight], axis=0)
        for j in range(rows // 16):
            pay[way * rows + 16 * j : way * rows + 16 * j + 16, width:] = pair


def states(heads, idx, slots, pieces, wx, wb, wd, bias, held, xa, ba, da, kx, kb, segs, rates):
    rows, part, depth = 2 * xa.shape[0], max(p.shape[0] for p in pieces), pieces[0].shape[1]
    nx, nb = wx.shape[1], wb.shape[1]
    blocks = rows // BLOCK
    plan, n = plan_of(pieces)
    return pl.pallas_call(
        functools.partial(state_kernel, heads, slots, plan),
        in_specs=[SMEM] + [ANY] * (len(pieces) + 2) + [VMEM] * 12,
        out_shape=[
            pltpu.HBM((rows, nx), BF16),
            pltpu.HBM((rows, nb), BF16),
            pltpu.HBM((SUB, rows), F32),
            pltpu.HBM((2 * LANES, nx + LANES), BF16),
            pltpu.HBM((2, blocks, LANES, nx), F32),
            pltpu.HBM((2, blocks, nx), F32),
        ],
        out_specs=[VMEM] * 6,
        scratch_shapes=scratch_of(n, part, depth, (nx, nb), 2 * n + len(pieces))
        + [pltpu.VMEM((rows + 16, nx), F32), pltpu.VMEM((rows + 16, nb), F32)],
        compiler_params=params(30),
        name="states",
    )(idx, *far(*pieces, wx, wb), wd, bias, *held, xa, ba, da, kx, kb, segs, rates)


def scan_kernel(heads, flag, src, out):
    count = src.shape[0]
    width = out.shape[2]
    ahead = flag[0] == 1

    def one(i, state):
        q = jnp.where(ahead, i, count - 1 - i)
        out[q] = state.astype(BF16)
        got = src[q].astype(F32)
        d = jnp.concatenate(
            [got[h : h + 1, width:] + got[heads + h : heads + h + 1, width:] for h in range(heads)], axis=1
        )
        return d * state + got[:, :width]

    lax.fori_loop(0, count, one, jnp.zeros((out.shape[1], width), F32), unroll=4)


def scan(heads, flag, src, width):
    return pl.pallas_call(
        functools.partial(scan_kernel, heads),
        in_specs=[pl.BlockSpec(memory_space=pltpu.SMEM), pl.BlockSpec(memory_space=pltpu.VMEM)],
        out_shape=jax.ShapeDtypeStruct((src.shape[0], src.shape[1], width), BF16),
        compiler_params=params(4),
        name="scan",
    )(flag, src)


def inside_kernel(heads, xs, bcs, dts, segs, rates, out):
    dt = dts[...]
    cf, ce = running(dt, rates[...][:, 0:1])
    row = segs[...]
    col = columns(cf, ce, row)
    bc = bcs[...]
    scores = nt_dot(bc[:, LANES:], bc[:, :LANES])
    scores = jnp.where(col[:, 2 * SUB : 2 * SUB + 1] == row[0:1], scores, 0.0)
    at, to = order()
    lower = to <= at
    x = xs[...]
    for h in range(heads):
        gap = jnp.where(lower, col[:, h : h + 1] - cf[h : h + 1], ce[h : h + 1] - col[:, SUB + h : SUB + h + 1])
        w = (scores * jnp.exp(gap) * dt[h : h + 1]).astype(BF16)
        out[:, h * LANES : (h + 1) * LANES] = dot(w, x[:, h * LANES : (h + 1) * LANES])


def row_block(width):
    return pl.BlockSpec((BLOCK, width), lambda b: (b, 0))


LANE_BLOCK = pl.BlockSpec((SUB, BLOCK), lambda b: (0, b))
RATE_BLOCK = pl.BlockSpec((SUB, LANES), lambda b: (0, 0))


def inside(heads, xs, bcs, dts, segs, rates):
    rows, nx = xs.shape
    nb = bcs.shape[1]
    return pl.pallas_call(
        functools.partial(inside_kernel, heads),
        grid=(rows // BLOCK,),
        in_specs=[row_block(nx), row_block(nb), LANE_BLOCK, LANE_BLOCK, RATE_BLOCK],
        out_specs=row_block(nx),
        out_shape=pltpu.HBM((rows, nx), F32),
        compiler_params=params(8),
        cost_estimate=pl.CostEstimate(
            flops=2 * rows * BLOCK * (nx + LANES), bytes_accessed=rows * nx * 6, transcendentals=rows * BLOCK * heads
        ),
        name="inside",
    )(*far(xs, bcs, dts), segs, rates)


def finish_kernel(heads, enter, loc, dec, y_in, sg, bcs, dts, segs, rates, out, ss):
    b = pl.program_id(0)
    cf, ce = running(dts[...], rates[...][:, 0:1])
    seg, prev, nxt, start, end, prev_end, next_start = marks(segs[...])
    col = columns(
        jnp.exp(cf) * equal(seg, prev_end), jnp.exp(cf[:, BLOCK - 1 :] - ce) * equal(seg, next_start)
    )
    c = bcs[...][:, LANES:]
    y = y_in[...]
    for way in range(2):
        held = dec[way, b][None] * enter[way * LANES : (way + 1) * LANES].astype(F32) + loc[way, 0]
        y = y + weigh(dot(c, held.astype(BF16)), col, way * SUB, heads)
    gated = y * sg[...]
    out[...] = gated
    sq = gated * gated
    part = sq[:, :LANES]
    for h in range(1, heads):
        part = part + sq[:, h * LANES : (h + 1) * LANES]
    ss[0] = jnp.sum(part.T, axis=0, keepdims=True)


def finish(heads, enter, loc, dec, y_in, sg, bcs, dts, segs, rates):
    rows, nx = y_in.shape
    nb = bcs.shape[1]
    blocks = rows // BLOCK
    return pl.pallas_call(
        functools.partial(finish_kernel, heads),
        grid=(blocks,),
        in_specs=[
            pl.BlockSpec(enter.shape, lambda b: (0, 0)),
            pl.BlockSpec((2, 1, LANES, nx), lambda b: (0, b, 0, 0)),
            pl.BlockSpec(dec.shape, lambda b: (0, 0, 0)),
            row_block(nx),
            row_block(nx),
            row_block(nb),
            LANE_BLOCK,
            LANE_BLOCK,
            RATE_BLOCK,
        ],
        out_specs=[row_block(nx), pl.BlockSpec((1, 1, BLOCK), lambda b: (b, 0, 0))],
        out_shape=[jax.ShapeDtypeStruct((rows, nx), F32), jax.ShapeDtypeStruct((blocks, 1, BLOCK), F32)],
        compiler_params=params(12),
        name="finish",
    )(enter, *far(loc, dec, y_in, sg, bcs, dts), segs, rates)


def scale_kernel(columns, gated, gain, *refs):
    parts, out = refs[:-1], refs[-1]
    total = parts[0][0]
    for p in parts[1:]:
        total = total + p[0]
    scale = lax.rsqrt(total / columns + 1e-05)
    col = jnp.broadcast_to(scale, (LANES, BLOCK)).T[:, 0:1]
    out[...] = (gated[...] * col * gain[...]).astype(BF16)


def scale(columns, gated, gain, parts):
    rows, nx = gated.shape
    row = pl.BlockSpec((BLOCK, nx), lambda b: (b, 0))
    part = pl.BlockSpec((1, 1, BLOCK), lambda b: (b, 0, 0))
    return pl.pallas_call(
        functools.partial(scale_kernel, columns),
        grid=(rows // BLOCK,),
        in_specs=[row, pl.BlockSpec((1, nx), lambda b: (0, 0))] + [part] * len(parts),
        out_specs=row,
        out_shape=jax.ShapeDtypeStruct((rows, nx), BF16),
        compiler_params=params(8),
        name="scale",
    )(gated, gain, *parts)


def tie(value, *after):
    return lax.optimization_barrier((value, *after))[0]


def shards(tokens, segment_ids, w_x, w_z, w_bc, w_dt, dt_bias, rates, conv_x, conv_bc, norm_gain):
    rows, depth = tokens.shape
    heads = w_dt.shape[1]
    nx = w_x.shape[1]
    mp, seq = lax.axis_size("mp"), lax.axis_size("seq")
    ring = mp // 2
    me = lax.axis_index("mp")
    row_at, col_at = me // ring, me % ring
    turn = lambda s: [(r * ring + c, r * ring + (c + s) % ring) for r in range(2) for c in range(ring)]
    send = lambda v, pairs: lax.ppermute(v, "mp", pairs)
    right, left = turn(1), turn(-1)
    across = [(i, (i + ring) % mp) for i in range(mp)]
    half = rows // 2

    def spread_out(own):
        cut = half // 2
        r1, l1, p = send(own, right), send(own, left), send(own, across)
        o1, o2 = send(r1[:cut], right), send(l1[cut:], left)
        pr, pm = send(p, right), send(p, left)
        return [own, r1, l1, p, o1, o2, pr, pm, send(o1, across), send(o2, across)]

    pieces_a = spread_out(tokens[:half])

    seg = segment_ids.astype(F32) + 1.0
    label = lambda v: jnp.broadcast_to(v[:, None], (SUB, LANES)).astype(BF16)
    tail = jnp.concatenate([tokens[rows - SUB :], label(seg[rows - SUB :])], axis=1)
    head = jnp.concatenate([tokens[:SUB], label(seg[:SUB])], axis=1)
    before = lax.ppermute(tail, "seq", [(i, i + 1) for i in range(seq - 1)])
    after = lax.ppermute(head, "seq", [(i + 1, i) for i in range(seq - 1)])
    left_seg = before[SUB - 1, depth].astype(F32)
    right_seg = after[0, depth].astype(F32)

    pieces_b = spread_out(jnp.concatenate([tokens[half:], before[:, :depth], after[:, :depth]], axis=0))
    idx = jnp.stack(
        [r * ring + (col_at + s) % ring for r, s in (
            (row_at, 0), (row_at, -1), (row_at, 1), (1 - row_at, 0),
            (row_at, 2), (1 - row_at, -1), (1 - row_at, 1), (1 - row_at, 2))]
    ).astype(jnp.int32)

    joined = jnp.concatenate([left_seg[None], seg, right_seg[None]])
    segs = jnp.stack([joined[1:-1], joined[:-2], joined[2:]] + [seg] * (SUB - 3))
    tall = lambda v, n: jnp.broadcast_to(jnp.pad(v, (0, n - heads))[:, None], (n, LANES))
    rate, bias = tall(rates, SUB), tall(dt_bias, 16)
    w_d = jnp.pad(w_dt.T, ((0, 16 - heads), (0, 0)))

    xa, ba, da = project(idx, tuple(range(8)), pieces_a, w_x, w_bc, w_d, bias, True)
    held = project(idx, (0, 1, 2, 3), pieces_b[:4], w_x, w_bc, w_d, bias, False)
    xs, bcs, dts, pay, loc, dec = states(
        heads, idx, (4, 5, 6, 7), pieces_b[4:], w_x, w_bc, w_d, bias, held, xa, ba, da, conv_x, conv_bc, segs, rate
    )

    width = nx
    got = lax.all_to_all(pay.reshape(seq, 2 * LANES // seq, width + LANES), "seq", 0, 0)
    flag = (lax.axis_index("seq") < seq // 2).astype(jnp.int32)[None]
    y_in = inside(heads, xs, bcs, dts, segs, rate)
    got, y_in = lax.optimization_barrier((got, y_in))
    entered = scan(heads, flag, got, width)
    enter = lax.all_to_all(entered, "seq", 0, 0).reshape(2 * LANES, width)
    sg = gate_project(idx, pieces_a, pieces_b, w_z)

    gated, ss = finish(heads, enter, loc, dec, y_in, sg, bcs, dts, segs, rate)
    ss = ss + send(ss, across)
    parts = [ss] + [send(ss, turn(s)) for s in range(1, ring)]
    return scale(nx * mp, gated, norm_gain[None], parts)


def solution(mesh):
    placed = (
        P("seq", "mp"),
        P("seq"),
        P(None, "mp"),
        P(None, "mp"),
        P(),
        P(None, "mp"),
        P("mp"),
        P("mp"),
        P(None, "mp"),
        P(),
        P("mp"),
    )
    return jax.shard_map(
        shards, mesh=mesh, in_specs=placed, out_specs=P("seq", "mp"), check_vma=False
    )
```

```python
import functools

import jax
import jax.numpy as jnp
from jax import lax
from jax.experimental import pallas as pl
from jax.experimental.pallas import tpu as pltpu
from jax.sharding import PartitionSpec as P

BF16 = jnp.bfloat16
F32 = jnp.float32
BLOCK = 256
LANES = 128
SUB = 8
ANY = pl.BlockSpec(memory_space=pl.ANY)
VMEM = pl.BlockSpec(memory_space=pltpu.VMEM)
SMEM = pl.BlockSpec(memory_space=pltpu.SMEM)


def silu(v):
    half = 0.5 * v
    return half + half * jnp.tanh(half)


def dot(a, b):
    return jnp.dot(a, b, preferred_element_type=F32)


def params(mib):
    return pltpu.CompilerParams(vmem_limit_bytes=mib << 20)


def far(*arrays):
    return [pltpu.with_memory_space_constraint(a, pltpu.HBM) for a in arrays]


def fetch(pairs, sems):
    copies = [pltpu.make_async_copy(src, dst, sems.at[i]) for i, (src, dst) in enumerate(pairs)]
    for c in copies:
        c.start()
    return copies


def rows_of(ref, idx, k, depth):
    return ref.at[pl.ds(pl.multiple_of(idx[k] * depth, depth), depth)]


def nt_dot(a, b):
    return lax.dot_general(a, b, (((1,), (1,)), ((), ())), preferred_element_type=F32)


def place(plan, pieces, buf):
    return [(slot, ref, buf.at[slot, pl.ds(at, rows)]) for ref, (slot, at, rows) in zip(pieces, plan)]


def plan_of(pieces, keep=None):
    whole = max(p.shape[0] for p in pieces)
    full = keep or whole
    plan, slot, at = [], 0, 0
    for p in pieces:
        rows = min(p.shape[0], full - at)
        plan.append((slot, at, rows))
        at += p.shape[0]
        if at == whole:
            slot, at = slot + 1, 0
    return tuple(plan), slot


def multiply(slots, plan, idx, pieces, weights, wd, buf, views, sems, sums):
    depth = buf.shape[2]
    order_of = [[] for _ in slots]
    pairs = []
    for i, k in enumerate(slots):
        for w, v in zip(weights, views):
            order_of[i].append(len(pairs))
            pairs.append((rows_of(w, idx, k, depth), v.at[i]))
        for ref, (slot, at, rows) in zip(pieces, plan):
            if slot == i:
                order_of[i].append(len(pairs))
                pairs.append((ref.at[pl.ds(0, rows)], buf.at[i, pl.ds(at, rows)]))
    copies = fetch(pairs, sems)
    for i, k in enumerate(slots):
        for c in order_of[i]:
            copies[c].wait()
        lhs = buf[i]
        parts = [dot(lhs, v[i]) for v in views]
        if wd is not None:
            parts.append(nt_dot(wd[:, pl.ds(pl.multiple_of(idx[k] * depth, depth), depth)], lhs))
        sums = [p if s is None else s + p for s, p in zip(sums, parts)]
    return sums


def step_sizes(v, bias):
    v = v[:SUB] + bias[:SUB]
    return jnp.maximum(v, 0.0) + jnp.log1p(jnp.exp(-jnp.abs(v)))


def project_kernel(slots, plan, last, idx, *refs):
    n = len(plan)
    pieces, refs = refs[:n], refs[n:]
    wx, wb, wd, bias = refs[:4]
    held, refs = (refs[4:7], refs[7:]) if last else (None, refs[4:])
    outs, (buf, vx, vb, sems) = refs[:3], refs[3:]
    sums = [h[...] for h in held] if last else [None] * 3
    sums = multiply(slots, plan, idx, pieces, (wx, wb), wd, buf, (vx, vb), sems, sums)
    if last:
        outs[0][...] = sums[0].astype(BF16)
        outs[1][...] = sums[1].astype(BF16)
        outs[2][...] = step_sizes(sums[2], bias[...][:, 0:1])
    else:
        for o, s in zip(outs, sums):
            o[...] = s


def scratch_of(n, rows, depth, widths, copies):
    return (
        [pltpu.VMEM((n, rows, depth), BF16)]
        + [pltpu.VMEM((n, depth, w), BF16) for w in widths]
        + [pltpu.SemaphoreType.DMA((copies,))]
    )


def project(idx, slots, pieces, wx, wb, wd, bias, held=()):
    last = len(held) > 0
    rows, depth = max(p.shape[0] for p in pieces), pieces[0].shape[1]
    plan, n = plan_of(pieces)
    nx, nb, nd = wx.shape[1], wb.shape[1], wd.shape[0]
    kind = BF16 if last else F32
    return pl.pallas_call(
        functools.partial(project_kernel, slots, plan, last),
        in_specs=[SMEM] + [ANY] * (len(pieces) + 2) + [VMEM] * (2 + len(held)),
        out_specs=[VMEM] * 3,
        scratch_shapes=scratch_of(n, rows, depth, (nx, nb), 2 * n + len(pieces)),
        out_shape=[
            jax.ShapeDtypeStruct((rows, nx), kind),
            jax.ShapeDtypeStruct((rows, nb), kind),
            jax.ShapeDtypeStruct((SUB if last else nd, rows), F32),
        ],
        compiler_params=params(24),
        cost_estimate=pl.CostEstimate(
            flops=2 * rows * depth * n * (nx + nb + LANES),
            bytes_accessed=2 * depth * n * (rows + nx + nb),
            transcendentals=0,
        ),
        name="project",
    )(idx, *far(*pieces, wx, wb), wd, bias, *held)


def gate_kernel(plan_a, plan_b, idx, *refs):
    na, nb = len(plan_a), len(plan_b)
    pieces_a, pieces_b, (wz, out, buf, vz, sems) = refs[:na], refs[na : na + nb], refs[na + nb :]
    half = out.shape[0] // 2
    n, depth = buf.shape[0], buf.shape[2]
    plan = [(s, at, r) for s, at, r in plan_a] + [(s, at + half, r) for s, at, r in plan_b]
    (total,) = multiply(
        tuple(range(n)), plan, idx, pieces_a + pieces_b, (wz,), None, buf, (vz,), sems, [None]
    )
    out[...] = silu(total.astype(BF16).astype(F32))


def gate_project(idx, pieces_a, pieces_b, wz):
    half, depth = pieces_a[0].shape
    nz = wz.shape[1]
    plan_a, n = plan_of(pieces_a)
    plan_b, _ = plan_of(pieces_b, half)
    count = len(plan_a) + len(plan_b)
    return pl.pallas_call(
        functools.partial(gate_kernel, plan_a, plan_b),
        in_specs=[SMEM] + [ANY] * (count + 1),
        out_specs=VMEM,
        scratch_shapes=scratch_of(n, 2 * half, depth, (nz,), n + count),
        out_shape=pltpu.HBM((2 * half, nz), F32),
        compiler_params=params(28),
        cost_estimate=pl.CostEstimate(
            flops=4 * half * depth * n * nz, bytes_accessed=2 * depth * n * (2 * half + nz), transcendentals=0
        ),
        name="gate",
    )(idx, *far(*pieces_a, *pieces_b, wz))


def order(strict=False):
    at = lax.broadcasted_iota(jnp.int32, (BLOCK, BLOCK), 0)
    to = lax.broadcasted_iota(jnp.int32, (BLOCK, BLOCK), 1)
    return at, to


def running(dt, rates):
    at, to = order()
    a = -dt * rates
    rows = a.shape[0]
    high = a.astype(BF16)
    rest = a - high.astype(F32)
    mid = rest.astype(BF16)
    low = (rest - mid.astype(F32)).astype(BF16)
    three = dot(jnp.concatenate([high, mid, low], axis=0), (at <= to).astype(F32).astype(BF16))
    cf = three[:rows] + three[rows : 2 * rows] + three[2 * rows :]
    return cf, cf - a


def columns(*groups):
    zero = jnp.zeros((LANES - SUB * len(groups), BLOCK), F32)
    return jnp.concatenate([*groups, zero], axis=0).T


def equal(a, b):
    return (a == b).astype(F32)


def marks(segs):
    seg, prev, nxt = segs[0:1], segs[1:2], segs[2:3]
    return seg, prev, nxt, seg[:, :1], seg[:, BLOCK - 1 :], prev[:, :1], nxt[:, BLOCK - 1 :]


def spread(col, heads):
    return jnp.concatenate([jnp.broadcast_to(col[h : h + 1], (1, LANES)) for h in range(heads)], axis=1)


def weigh(values, weights, at, heads):
    return jnp.concatenate(
        [values[:, h * LANES : (h + 1) * LANES] * weights[:, at + h : at + h + 1] for h in range(heads)], axis=1
    )


def state_kernel(heads, slots, plan, idx, *refs):
    n = len(plan)
    pieces, refs = refs[:n], refs[n:]
    wx, wb, wd, bias, hx, hb, hd, xa, ba, da, kx, kb, segs, rates = refs[:14]
    xs, bcs, dts, sums_out, opens, pay, loc_out, dec = refs[14:22]
    buf, vx, vb, sems, xf, bf, loc = refs[22:]
    half = xa.shape[0]
    blocks = 2 * half // BLOCK
    xf[8 : 8 + half] = xa[...].astype(F32)
    bf[8 : 8 + half] = ba[...].astype(F32)
    sums = multiply(slots, plan, idx, pieces, (wx, wb), wd, buf, (vx, vb), sems, [hx[...], hb[...], hd[...]])
    for dst, full in ((xf, sums[0]), (bf, sums[1])):
        full = full.astype(BF16).astype(F32)
        dst[8 + half : 8 + 2 * half] = full[:half]
        edge = full[half:]
        dst[7:8] = edge[SUB - 1 : SUB]
        dst[8 + 2 * half : 9 + 2 * half] = edge[SUB : SUB + 1]
    dts[:, :half] = da[...]
    dts[:, half:] = step_sizes(sums[2], bias[...][:, 0:1])[:, :half]
    rate = rates[...][:, 0:1]
    cut = lambda ref, b: ref[:, b * BLOCK : (b + 1) * BLOCK]
    cfs, ces = running(
        jnp.concatenate([cut(dts, b) for b in range(blocks)], axis=0), jnp.concatenate([rate] * blocks, axis=0)
    )
    steps = []
    for b in range(blocks):
        at = b * BLOCK
        seg, prev, nxt, start, end, prev_end, next_start = marks(segs[:, at : at + BLOCK])
        dt = dts[:, at : at + BLOCK]
        cf, ce = cfs[SUB * b : SUB * (b + 1)], ces[SUB * b : SUB * (b + 1)]
        last = cf[:, BLOCK - 1 :]
        sums_out[:, at : at + BLOCK] = jnp.concatenate([cf, ce], axis=0)
        opens[:, at : at + BLOCK] = jnp.concatenate(
            [jnp.exp(cf) * equal(seg, prev_end), jnp.exp(last - ce) * equal(seg, next_start)], axis=0
        )
        wide = lambda row: jnp.broadcast_to(row, (SUB, BLOCK))
        col = columns(
            jnp.exp(last - cf) * dt * equal(seg, end),
            jnp.exp(ce) * dt * equal(seg, start),
            wide(equal(seg, prev)),
            wide(equal(seg, nxt)),
        )
        steps.append((jnp.exp(last) * equal(end, prev_end), jnp.exp(last) * equal(start, next_start)))
        same_prev, same_next = col[:, 2 * SUB : 2 * SUB + 1], col[:, 3 * SUB : 3 * SUB + 1]

        def conv(src, taps):
            base = 8 + at
            before = src[base - 1 : base - 1 + BLOCK] * same_prev
            after = src[base + 1 : base + 1 + BLOCK] * same_next
            return silu(taps[0:1] * before + taps[1:2] * src[base : base + BLOCK] + taps[2:3] * after)

        x_blk = conv(xf, kx).astype(BF16)
        bc_blk = conv(bf, kb).astype(BF16)
        xs[at : at + BLOCK] = x_blk
        bcs[at : at + BLOCK] = bc_blk
        x_f = x_blk.astype(F32)
        b_t = bc_blk[:, :LANES].astype(F32).T.astype(BF16)
        loc[0, b] = dot(b_t, weigh(x_f, col, 0, heads).astype(BF16))
        loc[1, b] = dot(b_t, weigh(x_f, col, SUB, heads).astype(BF16))
    for way in range(2):
        total = jnp.ones((SUB, 1), F32)
        state = jnp.zeros((loc.shape[2], loc.shape[3]), F32)
        for i in range(blocks):
            b = i if way == 0 else blocks - 1 - i
            fresh = loc[way, b]
            loc_out[way, b] = state.astype(BF16)
            dec[way, b : b + 1] = spread(total, heads)
            step = steps[b][way]
            state = spread(step, heads) * state + fresh
            total = total * step
        rows, width = state.shape
        pay[way * rows : (way + 1) * rows, :width] = state.astype(BF16)
        high = total[:heads].astype(BF16).astype(F32)
        both = jnp.concatenate([high, total[:heads] - high], axis=0)
        eight = jnp.broadcast_to(both, (2 * heads, LANES)).astype(BF16)
        pair = jnp.concatenate([eight, eight], axis=0)
        for j in range(rows // 16):
            pay[way * rows + 16 * j : way * rows + 16 * j + 16, width:] = pair


def states(heads, idx, slots, pieces, wx, wb, wd, bias, held, xa, ba, da, kx, kb, segs, rates):
    rows, part, depth = 2 * xa.shape[0], max(p.shape[0] for p in pieces), pieces[0].shape[1]
    nx, nb = wx.shape[1], wb.shape[1]
    blocks = rows // BLOCK
    plan, n = plan_of(pieces)
    return pl.pallas_call(
        functools.partial(state_kernel, heads, slots, plan),
        in_specs=[SMEM] + [ANY] * (len(pieces) + 2) + [VMEM] * 12,
        out_shape=[
            pltpu.HBM((rows, nx), BF16),
            pltpu.HBM((rows, nb), BF16),
            pltpu.HBM((SUB, rows), F32),
            pltpu.HBM((2 * SUB, rows), F32),
            pltpu.HBM((2 * SUB, rows), F32),
            pltpu.HBM((2 * LANES, nx + LANES), BF16),
            pltpu.HBM((2, blocks, LANES, nx), BF16),
            pltpu.HBM((2, blocks, nx), F32),
        ],
        out_specs=[VMEM] * 8,
        scratch_shapes=scratch_of(n, part, depth, (nx, nb), 2 * n + len(pieces))
        + [
            pltpu.VMEM((rows + 16, nx), F32),
            pltpu.VMEM((rows + 16, nb), F32),
            pltpu.VMEM((2, blocks, LANES, nx), F32),
        ],
        compiler_params=params(30),
        name="states",
    )(idx, *far(*pieces, wx, wb), wd, bias, *held, xa, ba, da, kx, kb, segs, rates)


def scan_kernel(heads, flag, src, out):
    count = src.shape[0]
    width = out.shape[2]
    ahead = flag[0] == 1

    def one(i, state):
        q = jnp.where(ahead, i, count - 1 - i)
        out[q] = state.astype(BF16)
        got = src[q].astype(F32)
        d = jnp.concatenate(
            [got[h : h + 1, width:] + got[heads + h : heads + h + 1, width:] for h in range(heads)], axis=1
        )
        return d * state + got[:, :width]

    lax.fori_loop(0, count, one, jnp.zeros((out.shape[1], width), F32), unroll=4)


def scan(heads, flag, src, width):
    return pl.pallas_call(
        functools.partial(scan_kernel, heads),
        in_specs=[pl.BlockSpec(memory_space=pltpu.SMEM), pl.BlockSpec(memory_space=pltpu.VMEM)],
        out_shape=jax.ShapeDtypeStruct((src.shape[0], src.shape[1], width), BF16),
        compiler_params=params(4),
        name="scan",
    )(flag, src)


def inside_kernel(heads, xs, bcs, dts, sums, segs, out):
    dt = dts[...]
    cf, ce = sums[:SUB], sums[SUB:]
    row = segs[...]
    col = columns(cf, ce, row)
    bc = bcs[...]
    scores = nt_dot(bc[:, LANES:], bc[:, :LANES])
    scores = jnp.where(col[:, 2 * SUB : 2 * SUB + 1] == row[0:1], scores, 0.0)
    at, to = order()
    lower = to <= at
    x = xs[...]
    for h in range(heads):
        gap = jnp.where(lower, col[:, h : h + 1] - cf[h : h + 1], ce[h : h + 1] - col[:, SUB + h : SUB + h + 1])
        w = (scores * jnp.exp(gap) * dt[h : h + 1]).astype(BF16)
        out[:, h * LANES : (h + 1) * LANES] = dot(w, x[:, h * LANES : (h + 1) * LANES])


def row_block(width):
    return pl.BlockSpec((BLOCK, width), lambda b: (b, 0))


LANE_BLOCK = pl.BlockSpec((SUB, BLOCK), lambda b: (0, b))
PAIR_BLOCK = pl.BlockSpec((2 * SUB, BLOCK), lambda b: (0, b))


def inside(heads, xs, bcs, dts, sums, segs):
    rows, nx = xs.shape
    nb = bcs.shape[1]
    return pl.pallas_call(
        functools.partial(inside_kernel, heads),
        grid=(rows // BLOCK,),
        in_specs=[row_block(nx), row_block(nb), LANE_BLOCK, PAIR_BLOCK, LANE_BLOCK],
        out_specs=row_block(nx),
        out_shape=pltpu.HBM((rows, nx), F32),
        compiler_params=params(8),
        cost_estimate=pl.CostEstimate(
            flops=2 * rows * BLOCK * (nx + LANES), bytes_accessed=rows * nx * 6, transcendentals=rows * BLOCK * heads
        ),
        name="inside",
    )(*far(xs, bcs, dts, sums), segs)


def finish_kernel(heads, enter, loc, dec, y_in, sg, bcs, opens, out, ss):
    b = pl.program_id(0)
    col = columns(opens[:SUB], opens[SUB:])
    c = bcs[...][:, LANES:]
    y = y_in[...]
    for way in range(2):
        held = dec[way, b][None] * enter[way * LANES : (way + 1) * LANES].astype(F32) + loc[way, 0].astype(F32)
        y = y + weigh(dot(c, held.astype(BF16)), col, way * SUB, heads)
    gated = y * sg[...]
    out[...] = gated
    sq = gated * gated
    part = sq[:, :LANES]
    for h in range(1, heads):
        part = part + sq[:, h * LANES : (h + 1) * LANES]
    ss[0] = jnp.sum(part.T, axis=0, keepdims=True)


def finish(heads, enter, loc, dec, y_in, sg, bcs, opens):
    rows, nx = y_in.shape
    nb = bcs.shape[1]
    blocks = rows // BLOCK
    return pl.pallas_call(
        functools.partial(finish_kernel, heads),
        grid=(blocks,),
        in_specs=[
            pl.BlockSpec(enter.shape, lambda b: (0, 0)),
            pl.BlockSpec((2, 1, LANES, nx), lambda b: (0, b, 0, 0)),
            pl.BlockSpec(dec.shape, lambda b: (0, 0, 0)),
            row_block(nx),
            row_block(nx),
            row_block(nb),
            PAIR_BLOCK,
        ],
        out_specs=[row_block(nx), pl.BlockSpec((1, 1, BLOCK), lambda b: (b, 0, 0))],
        out_shape=[jax.ShapeDtypeStruct((rows, nx), F32), jax.ShapeDtypeStruct((blocks, 1, BLOCK), F32)],
        compiler_params=params(12),
        name="finish",
    )(enter, *far(loc, dec, y_in, sg, bcs, opens))


def scale_kernel(columns, gated, gain, *refs):
    parts, out = refs[:-1], refs[-1]
    for i in range(out.shape[0] // BLOCK):
        total = parts[0][i]
        for p in parts[1:]:
            total = total + p[i]
        factor = lax.rsqrt(total / columns + 1e-05)
        col = jnp.broadcast_to(factor, (LANES, BLOCK)).T[:, 0:1]
        at = pl.ds(i * BLOCK, BLOCK)
        out[at] = (gated[at] * col * gain[...]).astype(BF16)


def scale(columns, gated, gain, parts):
    rows, nx = gated.shape
    per = 2
    row = pl.BlockSpec((per * BLOCK, nx), lambda b: (b, 0))
    part = pl.BlockSpec((per, 1, BLOCK), lambda b: (b, 0, 0))
    return pl.pallas_call(
        functools.partial(scale_kernel, columns),
        grid=(rows // (per * BLOCK),),
        in_specs=[row, pl.BlockSpec((1, nx), lambda b: (0, 0))] + [part] * len(parts),
        out_specs=row,
        out_shape=jax.ShapeDtypeStruct((rows, nx), BF16),
        compiler_params=params(8),
        name="scale",
    )(gated, gain, *parts)


def tie(value, *after):
    return lax.optimization_barrier((value, *after))[0]


def shards(tokens, segment_ids, w_x, w_z, w_bc, w_dt, dt_bias, rates, conv_x, conv_bc, norm_gain):
    rows, depth = tokens.shape
    heads = w_dt.shape[1]
    nx = w_x.shape[1]
    mp, seq = lax.axis_size("mp"), lax.axis_size("seq")
    ring = mp // 2
    me = lax.axis_index("mp")
    row_at, col_at = me // ring, me % ring
    turn = lambda s: [(r * ring + c, r * ring + (c + s) % ring) for r in range(2) for c in range(ring)]
    send = lambda v, pairs: lax.ppermute(v, "mp", pairs)
    right, left = turn(1), turn(-1)
    across = [(i, (i + ring) % mp) for i in range(mp)]
    half = rows // 2

    def hop(own):
        return own, send(own, right), send(own, left), send(own, across)

    def spread_out(own, r1, l1, p):
        cut = half // 2
        o1, o2 = send(r1[:cut], right), send(l1[cut:], left)
        o1, o2, q = lax.optimization_barrier((o1, o2, p))
        return [own, r1, l1, p, o1, o2, send(q, right), send(q, left), send(o1, across), send(o2, across)]

    hop_a = hop(tokens[:half])

    seg = segment_ids.astype(F32) + 1.0
    label = lambda v: jnp.broadcast_to(v[:, None], (SUB, LANES)).astype(BF16)
    tail = jnp.concatenate([tokens[rows - SUB :], label(seg[rows - SUB :])], axis=1)
    head = jnp.concatenate([tokens[:SUB], label(seg[:SUB])], axis=1)
    before = lax.ppermute(tail, "seq", [(i, i + 1) for i in range(seq - 1)])
    after = lax.ppermute(head, "seq", [(i + 1, i) for i in range(seq - 1)])
    left_seg = before[SUB - 1, depth].astype(F32)
    right_seg = after[0, depth].astype(F32)

    own_b = jnp.concatenate([tokens[half:], before[:, :depth], after[:, :depth]], axis=0)
    own_b, *hop_a = lax.optimization_barrier((own_b, *hop_a))
    pieces_a = spread_out(*hop_a)
    pieces_b = spread_out(*hop(own_b))
    idx = jnp.stack(
        [r * ring + (col_at + s) % ring for r, s in (
            (row_at, 0), (row_at, -1), (row_at, 1), (1 - row_at, 0),
            (row_at, 2), (1 - row_at, -1), (1 - row_at, 1), (1 - row_at, 2))]
    ).astype(jnp.int32)

    joined = jnp.concatenate([left_seg[None], seg, right_seg[None]])
    segs = jnp.stack([joined[1:-1], joined[:-2], joined[2:]] + [seg] * (SUB - 3))
    tall = lambda v, n: jnp.broadcast_to(jnp.pad(v, (0, n - heads))[:, None], (n, LANES))
    rate, bias = tall(rates, SUB), tall(dt_bias, 16)
    w_d = jnp.pad(w_dt.T, ((0, 16 - heads), (0, 0)))

    w_d = tie(w_d, pieces_a[4], pieces_a[5])
    held_a = project(idx, (0, 1, 2, 3), pieces_a[:4], w_x, w_bc, w_d, bias)
    w_d, *held_a = lax.optimization_barrier((w_d, *held_a, pieces_b[4], pieces_b[5]))[:4]
    xa, ba, da = project(idx, (4, 5, 6, 7), pieces_a[4:], w_x, w_bc, w_d, bias, held_a)
    held = project(idx, (0, 1, 2, 3), pieces_b[:4], w_x, w_bc, w_d, bias)
    xs, bcs, dts, sums, opens, pay, loc, dec = states(
        heads, idx, (4, 5, 6, 7), pieces_b[4:], w_x, w_bc, w_d, bias, held, xa, ba, da, conv_x, conv_bc, segs, rate
    )

    width = nx
    got = lax.all_to_all(pay.reshape(seq, 2 * LANES // seq, width + LANES), "seq", 0, 0)
    flag = (lax.axis_index("seq") < seq // 2).astype(jnp.int32)[None]
    y_in = inside(heads, xs, bcs, dts, sums, segs)
    got, y_in = lax.optimization_barrier((got, y_in))
    entered = scan(heads, flag, got, width)
    enter = lax.all_to_all(entered, "seq", 0, 0).reshape(2 * LANES, width)
    sg = gate_project(idx, pieces_a, pieces_b, w_z)

    gated, ss = finish(heads, enter, loc, dec, y_in, sg, bcs, opens)
    ss = ss + send(ss, across)
    parts = [ss] + [send(ss, turn(s)) for s in range(1, ring)]
    return scale(nx * mp, gated, norm_gain[None], parts)


def solution(mesh):
    placed = (
        P("seq", "mp"),
        P("seq"),
        P(None, "mp"),
        P(None, "mp"),
        P(),
        P(None, "mp"),
        P("mp"),
        P("mp"),
        P(None, "mp"),
        P(),
        P("mp"),
    )
    return jax.shard_map(
        shards, mesh=mesh, in_specs=placed, out_specs=P("seq", "mp"), check_vma=False
    )
```
